512 devices in a mesh: dp: 32 (over y, z_lo, core), expert: 16 (over x, z_hi).
Axes of the slice: x: 4, y: 4, z: 16 (z_hi: 4, z_lo: 4; z = z_hi * 4 + z_lo), core: 2. Of those that a mesh axis runs over, the one named last changes fastest.
Arguments:
- tokens: bfloat16 [65536, 2560], P(('dp', 'expert')), may hold values from -6 to 6
- cotangent: bfloat16 [65536, 2560], P(('dp', 'expert')), may hold values from -6 to 6
- routes: int32 [65536, 6], P(('dp', 'expert')), may hold values from 0 to 159, all different within a row
- gates: float32 [65536, 6], P(('dp', 'expert')), may hold values from 0.05 to 0.5
- layout: int32 [3, 16], replicated, may hold values from 0 to 15, as said below
- weights: bfloat16 [16, 2560, 768], P('expert', 'dp'), may hold values from -0.125 to 0.125
- first_moment: float32 [16, 2560, 768], P('expert', 'dp'), may hold values from -12 to 12
- second_moment: float32 [16, 2560, 768], P('expert', 'dp'), may hold values from 0.5 to 50
Outputs:
- grad_input: bfloat16 [65536, 2560], P(('dp', 'expert'))
- new_first: float32 [16, 2560, 768], P('expert', 'dp')
- new_second: float32 [16, 2560, 768], P('expert', 'dp')
The draws below stay inside these ranges and needn't reach their ends.
Inputs may be any that keep to these rules, and one draw needn't show every extreme that they name: `routes`: each token names 6 different experts. Row 0 is a permutation of the slots; row 1 is i XOR m for one m of 1 to 15, the same for every i, so that i and layout[1, i] form a pair; row 2 holds 0 or 1, equal for both members of a pair; some pair swaps and, where there are two pairs or more, some pair keeps its slots.
All inputs are finite; a program needn't handle non-finite values.
Results may differ from the reference program's by a relative error of at most 0.015.
Values may be sent and summed in bfloat16 or wider, within the bound.
A program may use at most 64 MiB of HBM per device.

```python
import math
import jax
import jax.numpy as jnp
from jax import lax

D = 2560
H = 1024
HSPLIT = 4
HD = 256
ROUTED = 160
TOPK = 6
TOK_DEV = 128
CAP = 8
TOKENS = 65536
N_DP = 32
N_EXPERT = 16


def draw_layout(key, part):
    base_key = jax.random.fold_in(key, 7)
    perm_key, mask_key, swap_key, other_key, coin_key = jax.random.split(base_key, 5)
    lane_ids = jnp.arange(N_EXPERT, dtype=jnp.int32)
    placement = jax.random.permutation(perm_key, lane_ids).astype(jnp.int32)
    xor_mask = jax.random.randint(mask_key, (), 1, N_EXPERT, dtype=jnp.int32)
    partner = jnp.bitwise_xor(lane_ids, xor_mask)
    lowest = jnp.minimum(lane_ids, partner)
    coins = jax.random.randint(coin_key, (N_EXPERT,), 0, 2, dtype=jnp.int32)
    swap_lane = jax.random.randint(swap_key, (), 0, N_EXPERT, dtype=jnp.int32)
    other = jax.random.randint(other_key, (), 1, N_EXPERT - 1, dtype=jnp.int32)
    other = other + (other >= xor_mask).astype(jnp.int32)
    keep_lane = jnp.bitwise_xor(swap_lane, other)
    coins = jnp.where(lane_ids == jnp.minimum(swap_lane, jnp.bitwise_xor(swap_lane, xor_mask)), 1, coins)
    coins = jnp.where(lane_ids == jnp.minimum(keep_lane, jnp.bitwise_xor(keep_lane, xor_mask)), 0, coins)
    switch = coins[lowest].astype(jnp.int32)
    return jnp.stack((placement, partner.astype(jnp.int32), switch))


def block_levels(own_key, extent, pieces, low, high):
    factor_of = 1.0
    for dim, blocks in pieces:
        heights = jax.random.uniform(jax.random.fold_in(jax.random.fold_in(own_key, 6), dim), (blocks,), jnp.float32, low / len(pieces), high / len(pieces))
        factor_of = factor_of * jnp.repeat(jnp.exp(heights), extent[dim] // blocks).reshape((-1,) + (1,) * (len(extent) - 1 - dim))
    return factor_of


def picks_of(rng, rows, number_of, top, lift):
    order = jax.random.permutation(jax.random.fold_in(rng, 1), number_of)
    pull = order
    for power in range(3):
        pull = pull * pull // number_of
    pull = pull * lift // number_of
    tickets = jax.random.randint(jax.random.fold_in(rng, 2), (rows, number_of), 0, 4096) + pull
    holders = jax.random.permutation(jax.random.fold_in(rng, 3), rows)[jnp.arange(number_of) % rows]
    tickets = jnp.where(jnp.arange(rows)[:, None] == holders[None, :], 1 << 14, tickets)
    merit = tickets * number_of + jnp.arange(number_of)
    return lax.top_k(merit.astype(jnp.int32), top)[1].astype(jnp.int32)


def noise(stream_key, dims, width, most, cuts=(), kind=jnp.bfloat16):
    drawn = width * jax.random.normal(stream_key, dims, jnp.float32)
    if cuts:
        drawn = drawn * block_levels(stream_key, dims, cuts, -0.22, 0.18)
    return jnp.clip(drawn, -most, most).astype(kind)


def setup_inputs(seed: int = 0) -> dict:
    splits = jax.random.split(jax.random.key(seed), 9)
    return {
        "tokens": noise(splits[0], (TOKENS, D), 1.0, 6.0, ((0, 512),)),
        "cotangent": noise(splits[1], (TOKENS, D), 1.0, 6.0, ((0, 512),)),
        "routes": picks_of(splits[2], TOKENS, ROUTED, TOPK, 307),
        "gates": jnp.clip(jnp.exp(math.log(0.5) - 2.3025851 * jax.random.uniform(splits[3], (TOKENS, TOPK), jnp.float32) ** block_levels(splits[3], (TOKENS, TOPK), ((0, 512),), -0.2, 0.2)), 0.05, 0.5),
        "layout": draw_layout(jax.random.fold_in(splits[8], 71), 0),
        "weights": noise(splits[5], (N_EXPERT, D, 3 * HD), D ** -0.5, 0.125, ((0, 16), (1, 32))),
        "first_moment": noise(splits[6], (N_EXPERT, D, 3 * HD), 2.0, 12.0, ((0, 16), (1, 32)), jnp.float32),
        "second_moment": jnp.clip(jnp.exp(math.log(50.0) - 4.6051702 * jax.random.uniform(splits[7], (N_EXPERT, D, 3 * HD), jnp.float32) ** block_levels(splits[7], (N_EXPERT, D, 3 * HD), ((0, 16), (1, 32)), -0.2, 0.2)), 0.5, 50.0),
    }


first_decay = 0.9
second_decay = 0.999


def rounded(values):
    return lax.optimization_barrier(values.astype(jnp.bfloat16)).astype(jnp.float32)


def take_rows(source, index_rows):
    return source[index_rows]


def add_rows(index_rows, values):
    return jnp.zeros((TOK_DEV + 1, D), jnp.float32).at[index_rows].add(values)


def reference(tokens, cotangent, routes, gates, layout, weights, first_moment, second_moment):
    placement = layout[0]
    xor_mask = layout[1, 0]
    swap_on = layout[2]
    n_block = N_DP * N_EXPERT
    n_window = N_EXPERT // HSPLIT
    width_dev = H // HSPLIT
    per_block = TOK_DEV * TOPK
    route_ids = routes.reshape(n_block, per_block)
    window_ids = jnp.arange(n_window, dtype=jnp.int32)
    hit_table = (route_ids[:, :, None] == window_ids[None, None, :]).astype(jnp.int32)
    earlier = jnp.cumsum(hit_table, axis=1) - hit_table
    position = jnp.sum(earlier * hit_table, axis=2)
    kept = (route_ids < n_window) & (position < CAP)
    slot_key = jnp.where(kept, route_ids * CAP + position, n_window * CAP).astype(jnp.int32)
    token_of = jnp.broadcast_to(jnp.arange(per_block, dtype=jnp.int32) // TOPK, (n_block, per_block))
    block_ids = jnp.broadcast_to(jnp.arange(n_block, dtype=jnp.int32)[:, None], (n_block, per_block))
    token_table = jnp.full((n_block, n_window * CAP + 1), TOK_DEV, dtype=jnp.int32)
    token_table = token_table.at[block_ids, slot_key].set(token_of)[:, :-1]
    gate_table = jnp.zeros((n_block, n_window * CAP + 1), jnp.float32)
    gate_table = gate_table.at[block_ids, slot_key].set(gates.reshape(n_block, per_block).astype(jnp.float32))[:, :-1]
    pad_rows = jnp.zeros((n_block, 1, D), jnp.bfloat16)
    token_blocks = jnp.concatenate((tokens.reshape(n_block, TOK_DEV, D), pad_rows), axis=1)
    cot_blocks = jnp.concatenate((cotangent.reshape(n_block, TOK_DEV, D), pad_rows), axis=1)
    x_buffer = jax.vmap(take_rows)(token_blocks, token_table).reshape(n_block, n_window, CAP, D)
    dy_rows = jax.vmap(take_rows)(cot_blocks, token_table).astype(jnp.float32) * gate_table[:, :, None]
    dy_buffer = dy_rows.astype(jnp.bfloat16).reshape(n_block, n_window, CAP, D)
    lane_ids = jnp.arange(N_EXPERT, dtype=jnp.int32)
    held_slot = jnp.where(swap_on == 1, jnp.bitwise_xor(lane_ids, xor_mask), lane_ids).astype(jnp.int32)
    inverse = jnp.zeros((N_EXPERT,), jnp.int32).at[placement].set(lane_ids)

    def per_slot(dx_total, slot_index):
        expert = (inverse[slot_index] // HSPLIT).astype(jnp.int32)
        w_full = weights[slot_index].astype(jnp.float32)
        rows_in = lax.dynamic_index_in_dim(x_buffer, expert, axis=1, keepdims=False)
        rows_in = rows_in.reshape(N_DP, N_EXPERT * CAP, D).astype(jnp.float32)
        grads_in = lax.dynamic_index_in_dim(dy_buffer, expert, axis=1, keepdims=False)
        grads_in = grads_in.reshape(N_DP, N_EXPERT * CAP, D).astype(jnp.float32)
        pre_act = jnp.einsum('ard,dh->arh', rows_in, w_full[:, :2 * width_dev], precision=lax.Precision.HIGHEST)
        hidden_grad = jnp.einsum('ard,dh->arh', grads_in, w_full[:, 2 * width_dev:], precision=lax.Precision.HIGHEST)
        gate_pre = pre_act[:, :, :width_dev]
        up_pre = pre_act[:, :, width_dev:]
        sigma = jax.nn.sigmoid(gate_pre)
        active_part = gate_pre * sigma
        hidden = rounded(active_part * up_pre)
        gate_grad = rounded(hidden_grad * up_pre * sigma * (1.0 + gate_pre * (1.0 - sigma)))
        up_grad = rounded(hidden_grad * active_part)
        both_grads = jnp.concatenate((gate_grad, up_grad), axis=2)
        part_rows = jnp.einsum('arh,dh->ard', both_grads, w_full[:, :2 * width_dev], precision=lax.Precision.HIGHEST)
        part_rows = rounded(part_rows).reshape(n_block, CAP, D)
        dx_total = dx_total.at[expert].add(part_rows)
        terms = jnp.concatenate((
            jnp.einsum('ard,arh->adh', rows_in, both_grads, precision=lax.Precision.HIGHEST),
            jnp.einsum('ard,arh->adh', grads_in, hidden, precision=lax.Precision.HIGHEST)), axis=2)
        weight_grad = jnp.sum(rounded(terms), axis=0)
        new_first = first_decay * first_moment[slot_index] + (1.0 - first_decay) * weight_grad
        new_second = second_decay * second_moment[slot_index] + (1.0 - second_decay) * weight_grad * weight_grad
        return dx_total, (new_first, new_second)

    start_total = jnp.zeros((n_window, n_block, CAP, D), jnp.float32)
    dx_total, (firsts, seconds) = lax.scan(per_slot, start_total, lane_ids)
    flat_parts = jnp.transpose(dx_total, (1, 0, 2, 3)).reshape(n_block, n_window * CAP, D)
    dx_blocks = jax.vmap(add_rows)(token_table, flat_parts)
    grad_input = dx_blocks[:, :TOK_DEV].reshape(TOKENS, D).astype(jnp.bfloat16)
    return grad_input, firsts[held_slot], seconds[held_slot]
```

```python
import jax
import jax.numpy as jnp
from jax import lax
from jax.sharding import Mesh
from jax.sharding import PartitionSpec as P

HSPLIT = 4
CAP = 8
AXES = ("y", "zl", "core", "x", "zh")
DP = ("y", "zl", "core")
EXPERT = ("x", "zh")
RING = ("zh", "zl")
PLANE = ("x", "y")
SPREAD = ("y", "core")

first_decay = 0.9
second_decay = 0.999


def partner_copy(block, mask, count):
    def branch(k):
        return lambda v: lax.ppermute(v, EXPERT, [(i, i ^ k) for i in range(count)])

    return lax.switch(mask - 1, [branch(k) for k in range(1, count)], block)


def local(tokens, cotangent, routes, gates, layout, weights, first_moment, second_moment):
    n_x, n_zh = lax.axis_size("x"), lax.axis_size("zh")
    n_y, n_zl, n_core = lax.axis_size("y"), lax.axis_size("zl"), lax.axis_size("core")
    n_expert = n_x * n_zh
    own_index = lax.axis_index(EXPERT)
    core = lax.axis_index("core")
    lane_ids = jnp.arange(n_expert, dtype=jnp.int32)
    placement = layout[0]
    mask = layout[1, 0]
    swap_on = layout[2]
    inverse = jnp.sum(
        jnp.where(placement[None, :] == lane_ids[:, None], lane_ids[None, :], 0), axis=1
    )
    slot_owner = inverse // HSPLIT
    active = jnp.sum(jnp.where(lane_ids == own_index, swap_on, 0)) == 1

    depth, wide = weights.shape[1:]
    half = wide // 3 // n_core
    w = weights[0].reshape(depth, 3, n_core, half).transpose(2, 0, 1, 3)
    w = w.reshape(n_core, depth, 3 * half)
    w = lax.all_gather(w, RING).reshape(n_zh, n_zl, n_core, depth, 3 * half)
    w = w.transpose(0, 2, 1, 3, 4).reshape(n_zh * n_core, n_zl, depth, 3 * half)
    w = lax.all_to_all(w, SPREAD, split_axis=0, concat_axis=0, tiled=True)
    w = w.reshape(n_y, n_core, n_zl, depth, 3 * half).transpose(0, 2, 1, 3, 4)
    w = w.reshape(-1, 3 * half)

    moments = jnp.stack((first_moment[0], second_moment[0]))
    moved = partner_copy(moments.astype(jnp.bfloat16), mask, n_expert)
    held = jnp.where(active, moved.astype(jnp.float32), moments)

    n_window = n_expert // HSPLIT
    tok_dev, top_count = routes.shape
    width = tokens.shape[1]
    flat_ids = routes.reshape(-1)
    window_ids = jnp.arange(n_window, dtype=jnp.int32)
    hit_table = (flat_ids[:, None] == window_ids[None, :]).astype(jnp.int32)
    earlier = jnp.cumsum(hit_table, axis=0) - hit_table
    position = jnp.sum(earlier * hit_table, axis=1)
    kept = (flat_ids < n_window) & (position < CAP)
    slot_key = jnp.where(kept, flat_ids * CAP + position, -1)
    slot_pick = (jnp.arange(n_window * CAP, dtype=jnp.int32)[:, None] == slot_key[None, :]).astype(
        jnp.float32
    )
    assign_rows = jnp.arange(tok_dev * top_count, dtype=jnp.int32)[:, None] // top_count
    assign_token = (assign_rows == jnp.arange(tok_dev, dtype=jnp.int32)[None, :]).astype(
        jnp.float32
    )
    slot_token = jnp.dot(slot_pick, assign_token, precision=lax.Precision.HIGHEST)
    slot_gate = jnp.dot(slot_pick, gates.reshape(-1), precision=lax.Precision.HIGHEST)
    choose = (slot_owner[:, None] == window_ids[None, :]).astype(jnp.float32)
    dest_token = jnp.dot(
        choose, slot_token.reshape(n_window, CAP * tok_dev), precision=lax.Precision.HIGHEST
    )
    dest_token = dest_token.reshape(n_expert * CAP, tok_dev).astype(jnp.bfloat16)
    dest_gate = jnp.dot(
        choose, slot_gate.reshape(n_window, CAP), precision=lax.Precision.HIGHEST
    ).reshape(-1, 1)
    send_rows = jnp.dot(dest_token, tokens, preferred_element_type=jnp.float32).astype(jnp.bfloat16)
    send_grads = (
        jnp.dot(dest_token, cotangent, preferred_element_type=jnp.float32) * dest_gate
    ).astype(jnp.bfloat16)
    send = jnp.concatenate(
        (send_rows.reshape(n_expert, CAP, width), send_grads.reshape(n_expert, CAP, width)), axis=1
    )
    got = lax.all_to_all(send, PLANE, split_axis=0, concat_axis=0, tiled=True)
    got = lax.all_gather(got, "core")
    rows_in = got[:, :, :CAP].reshape(-1, width)
    grads_in = got[:, :, CAP:].reshape(-1, width)

    pre_act = jnp.dot(rows_in, w[:, : 2 * half], preferred_element_type=jnp.float32)
    hidden_grad = jnp.dot(grads_in, w[:, 2 * half :], preferred_element_type=jnp.float32)
    gate_pre = pre_act[:, :half]
    up_pre = pre_act[:, half:]
    sigma = jax.nn.sigmoid(gate_pre)
    active_part = gate_pre * sigma
    hidden = (active_part * up_pre).astype(jnp.bfloat16)
    gate_grad = (hidden_grad * up_pre * sigma * (1.0 + gate_pre * (1.0 - sigma))).astype(
        jnp.bfloat16
    )
    up_grad = (hidden_grad * active_part).astype(jnp.bfloat16)
    both_grads = jnp.concatenate((gate_grad, up_grad), axis=1)

    proj_grad = lax.dot_general(
        rows_in, both_grads, (((0,), (0,)), ((), ())), preferred_element_type=jnp.float32
    )
    down_grad = lax.dot_general(
        grads_in, hidden, (((0,), (0,)), ((), ())), preferred_element_type=jnp.float32
    )
    g = jnp.concatenate((proj_grad, down_grad), axis=1).astype(jnp.bfloat16)
    g = g.reshape(n_y, n_zl, n_core, depth, 3 * half).transpose(0, 2, 1, 3, 4)
    g = g.reshape(n_y * n_core, n_zl, depth, 3 * half)
    g = lax.all_to_all(g, SPREAD, split_axis=0, concat_axis=0, tiled=True)
    g = g.reshape(n_zh, n_core, n_zl, depth, 3 * half).transpose(0, 2, 1, 3, 4)
    g = g.reshape(n_zh * n_zl * n_core * depth, 3 * half)

    part = lax.dot_general(
        both_grads,
        w[:, : 2 * half],
        (((1,), (1,)), ((), ())),
        preferred_element_type=jnp.float32,
    )
    part = part.astype(jnp.bfloat16).reshape(n_core, n_expert * CAP, width)
    theirs = jnp.where(core == 0, part[1], part[0])
    mine = jnp.where(core == 0, part[0], part[1])
    theirs = lax.ppermute(theirs, "core", [(0, 1), (1, 0)])
    part = (mine.astype(jnp.float32) + theirs.astype(jnp.float32)).astype(jnp.bfloat16)
    part = part.reshape(n_expert, CAP, width)
    returned = lax.all_to_all(part, PLANE, split_axis=0, concat_axis=0, tiled=True)
    grad_input = lax.dot_general(
        dest_token,
        returned.reshape(-1, width),
        (((0,), (0,)), ((), ())),
        preferred_element_type=jnp.float32,
    ).astype(jnp.bfloat16)

    g = lax.psum_scatter(g, RING, scatter_dimension=0, tiled=True)
    g = g.reshape(n_core, depth, 3, half).transpose(1, 2, 0, 3).reshape(depth, wide)
    g_moved = partner_copy(g, mask, n_expert)
    g = jnp.where(active, g_moved, g).astype(jnp.float32)
    new_first = first_decay * held[0] + (1.0 - first_decay) * g
    new_second = second_decay * held[1] + (1.0 - second_decay) * g * g
    return (grad_input, new_first[None], new_second[None])


def solution(mesh):
    split = Mesh(mesh.devices.reshape(4, 4, 2, 4, 4), AXES)
    rows = P(DP + EXPERT, None)
    slots = P(EXPERT, DP, None)
    return jax.shard_map(
        local,
        mesh=split,
        in_specs=(rows, rows, rows, rows, P(), slots, slots, slots),
        out_specs=(rows, slots, slots),
        check_vma=False,
    )
```
